32 devices in a mesh: row: 4 (over y, core), col: 8 (over z, x).
Axes of the slice: x: 2, y: 2, z: 4, core: 2. Of those that a mesh axis runs over, the one named last changes fastest.
Arguments:
- matrix: float32 [16, 4, 256, 8, 8, 256], P(None, 'row', None, None, 'col'), may hold values from -10 to 20, as said below
Outputs:
- factored: float32 [16, 4, 256, 8, 8, 256], P(None, 'row', None, None, 'col')
The draws below stay inside these ranges and needn't reach their ends.
Inputs may be any that keep to these rules, and one draw needn't show every extreme that they name: matrix is symmetric, and its leading 2 * 256 rows and columns form a positive definite block.
All inputs are finite; a program needn't handle non-finite values.
Results may differ from the reference program's by a relative error of at most 0.0001.
Values sent between devices are 32-bit elements; how exact they have to be, the bound alone decides.
A program may use at most 192 MiB of HBM per device.

```python
import jax
import jax.numpy as jnp
from jax import lax

N = 16384
NB = 256
STEPS = 2
KR = 16
KC = 8
N_ROW = 4
N_COL = 8


def draw_matrix(key, part):
    base = jax.random.fold_in(key, 11)
    first = jax.random.fold_in(base, 0)
    fourth = jax.random.fold_in(base, 3)
    leading = STEPS * NB
    random_part = jnp.clip(jax.random.normal(first, (N, N), jnp.float32), -4.0, 4.0)
    mixing = jnp.clip(jax.random.normal(fourth, (leading, leading), jnp.float32), -5.0, 5.0)
    symmetric = (random_part + random_part.T) * 0.7071
    gram = jnp.dot(mixing, mixing.T, precision=lax.Precision.HIGHEST) * (4.0 / leading)
    gram = (gram + gram.T) * 0.5
    dominant = gram + 4.0 * jnp.eye(leading, dtype=jnp.float32)
    symmetric = symmetric.at[:leading, :leading].set(dominant)
    return symmetric.reshape(KR, N_ROW, NB, KC, N_COL, NB)


def setup_inputs(seed: int = 0) -> dict:
    key_of = jax.random.split(jax.random.key(seed), 2)
    matrix = draw_matrix(jax.random.fold_in(key_of[1], 71), 0)
    return {"matrix": matrix}


def reference(matrix):
    full_matrix = matrix.reshape(N, N)
    identity = jnp.eye(NB, dtype=jnp.float32)
    row_index = jnp.arange(N)
    for section_at in range(STEPS):
        offset = section_at * NB
        diag_factor = jnp.linalg.cholesky(full_matrix[offset:offset + NB, offset:offset + NB])
        diag_inverse = jax.scipy.linalg.solve_triangular(diag_factor, identity, lower=True)
        factor_panel = jnp.dot(full_matrix[:, offset:offset + NB], diag_inverse.T, precision=lax.Precision.HIGHEST)
        factor_panel = jnp.where((row_index >= offset + NB)[:, None], factor_panel, jnp.zeros_like(factor_panel))
        full_matrix = full_matrix - jnp.dot(factor_panel, factor_panel.T, precision=lax.Precision.HIGHEST)
        column = factor_panel.at[offset:offset + NB].set(diag_factor)
        full_matrix = full_matrix.at[:, offset:offset + NB].set(column)
        full_matrix = full_matrix.at[offset:offset + NB, offset + NB:].set(jnp.zeros_like(full_matrix[offset:offset + NB, offset + NB:]))
    return full_matrix.reshape(matrix.shape)
```

```python
import functools

import jax
import jax.numpy as jnp
from jax import lax
from jax.experimental import pallas as pl
from jax.experimental.pallas import tpu as pltpu
from jax.sharding import PartitionSpec as P

LANES = 128
MESH_ID = pl.DeviceIdType.MESH
EXACT = lax.Precision.HIGHEST


def exchange(rows, cols, depth, m_ref, r_ref, c_ref, l_ref, ring_send, ring_recv,
             lead_send, lead_recv, wide_send, wide_recv, own_sem):
    row = lax.axis_index("row")
    col = lax.axis_index("col")
    half = cols // 2
    odd = lax.rem(col, 2)
    place = jnp.where(odd == 0, col // 2, cols - 1 - col // 2)

    def at(place):
        place = lax.rem(place + cols, cols)
        return jnp.where(place < half, 2 * place, 2 * (cols - 1 - place) + 1)

    after, before = at(place + 1), at(place - 1)
    barrier = pltpu.get_barrier_semaphore()
    for step in range(1, rows):
        pl.semaphore_signal(barrier, inc=1, device_id=(lax.rem(row + step, rows), col),
                            device_id_type=MESH_ID)
    for peer in (after, before):
        pl.semaphore_signal(barrier, inc=1, device_id=(row, peer), device_id_type=MESH_ID)
    pl.semaphore_wait(barrier, rows + 1)

    leads = ((0, 0), (1, 0), (1, 1))

    def lead_copy(index, step):
        return pltpu.make_async_remote_copy(
            src_ref=m_ref.at[0, :, 0], dst_ref=l_ref.at[index],
            send_sem=lead_send.at[index, step - 1], recv_sem=lead_recv.at[index],
            device_id=(lax.rem(row + step, rows), col), device_id_type=MESH_ID)

    def lead_own(index):
        return pltpu.make_async_copy(m_ref.at[0, :, 0], l_ref.at[index], own_sem.at[index])

    for index, (lead_row, lead_col) in enumerate(leads):
        @pl.when((row == lead_row) & (col == lead_col))
        def _():
            for step in range(1, rows):
                lead_copy(index, step).start()
            lead_own(index).start()

    def wide_copy(which, step):
        return pltpu.make_async_remote_copy(
            src_ref=m_ref.at[0], dst_ref=c_ref.at[which],
            send_sem=wide_send.at[which, step - 1], recv_sem=wide_recv.at[which],
            device_id=(lax.rem(row + step, rows), col), device_id_type=MESH_ID)

    def wide_own(which):
        return pltpu.make_async_copy(m_ref.at[0], c_ref.at[which], own_sem.at[3 + which])

    def column_own(which):
        return pltpu.make_async_copy(m_ref.at[:, :, 0], r_ref.at[which], own_sem.at[5 + which])

    for which in range(2):
        @pl.when(row == which)
        def _():
            for step in range(1, rows):
                wide_copy(which, step).start()
            wide_own(which).start()

        @pl.when(col == which)
        def _():
            column_own(which).start()

    for index, (lead_row, lead_col) in enumerate(leads):
        @pl.when((row != lead_row) & (col == lead_col))
        def _():
            lead_copy(index, 1).wait_recv()

        @pl.when((row == lead_row) & (col == lead_col))
        def _():
            lead_own(index).wait()

    streams = ((0, 1, 0), (0, -1, 1), (1, 1, 2), (1, -1, None))
    share = depth // 2

    def ring_copy(stream, chunk, first):
        source, way, lead = streams[stream]
        to = after if way == 1 else before
        if chunk == 0:
            src = dst = l_ref.at[lead]
        else:
            index = chunk - 1 + (share if way == -1 else 0)
            dst = r_ref.at[source, index]
            src = m_ref.at[index, :, 0] if first else dst
        return pltpu.make_async_remote_copy(
            src_ref=src, dst_ref=dst, send_sem=ring_send.at[stream, chunk],
            recv_sem=ring_recv.at[stream, chunk], device_id=(row, to),
            device_id_type=MESH_ID)

    starts = (0, cols - 1)
    away = [lax.rem(way * (place - starts[source]) + cols, cols)
            for source, way, _ in streams]
    for chunk in range(share + 1):
        for stream in range(len(streams)):
            if chunk == 0 and streams[stream][2] is None:
                continue

            @pl.when(away[stream] == 0)
            def _():
                ring_copy(stream, chunk, True).start()

            @pl.when(away[stream] > 0)
            def _():
                ring_copy(stream, chunk, False).wait_recv()

            @pl.when((away[stream] > 0) & (away[stream] < cols - 1))
            def _():
                ring_copy(stream, chunk, False).start()

    for chunk in range(share + 1):
        for stream in range(len(streams)):
            if chunk == 0 and streams[stream][2] is None:
                continue

            @pl.when(away[stream] < cols - 1)
            def _():
                ring_copy(stream, chunk, False).wait_send()

    for index, (lead_row, lead_col) in enumerate(leads):
        @pl.when((row == lead_row) & (col == lead_col))
        def _():
            for step in range(1, rows):
                lead_copy(index, step).wait_send()

    for which in range(2):
        @pl.when(row == which)
        def _():
            for step in range(1, rows):
                wide_copy(which, step).wait_send()
            wide_own(which).wait()

        @pl.when(row != which)
        def _():
            wide_copy(which, 1).wait_recv()

        @pl.when(col == which)
        def _():
            column_own(which).wait()


def split(value):
    high = value.astype(jnp.bfloat16)
    return high, (value - high.astype(jnp.float32)).astype(jnp.bfloat16)


def mul(a, b):
    return jnp.dot(a, b, precision=EXACT, preferred_element_type=jnp.float32)


def mul_t(a, b):
    return lax.dot_general(a, b, (((1,), (1,)), ((), ())), precision=EXACT,
                           preferred_element_type=jnp.float32)


def update(width, edge, r_ref, c_ref, f_ref, m_ref, o_ref, high_ref, low_ref):
    index = pl.program_id(0)
    row = lax.axis_index("row")
    col = lax.axis_index("col")
    parts = edge // LANES
    stride = width * parts
    inv0, low10, inv1 = f_ref[0], f_ref[1], f_ref[2]

    def tile(ref, lead, j):
        return jnp.concatenate(
            [ref[lead + (pl.ds(j * parts + h, edge, stride=stride), slice(None))]
             for h in range(parts)], axis=1)

    def put(j, value):
        for h in range(parts):
            o_ref[0, pl.ds(j * parts + h, edge, stride=stride), :] = (
                value[:, h * LANES:(h + 1) * LANES])

    @pl.when(index == 0)
    def _():
        for j in range(width):
            first = mul(inv0, tile(c_ref, (0,), j))
            second = mul(inv1, tile(c_ref, (1,), j) - mul(low10, first))
            here = slice(j * edge, (j + 1) * edge)
            for k, value in enumerate((first, second)):
                high, low = split(value)
                high_ref[k * edge:(k + 1) * edge, here] = high
                low_ref[k * edge:(k + 1) * edge, here] = low

    def column(which):
        return jnp.concatenate(
            [r_ref[which, 0, pl.ds(h, edge, stride=parts), :] for h in range(parts)], axis=1)

    first = mul_t(column(0), inv0)
    second = mul_t(column(1) - mul_t(first, low10), inv1)
    high, low = split(jnp.concatenate([first, second], axis=1))
    for j in range(width):
        here = slice(j * edge, (j + 1) * edge)
        wide_high, wide_low = high_ref[:, here], low_ref[:, here]
        change = jnp.dot(high, wide_low, preferred_element_type=jnp.float32)
        change += jnp.dot(low, wide_high, preferred_element_type=jnp.float32)
        change += jnp.dot(high, wide_high, preferred_element_type=jnp.float32)
        put(j, tile(m_ref, (0,), j) - change)

    @pl.when(col == 0)
    def _():
        put(0, first)

    @pl.when(col == 1)
    def _():
        put(0, second)

    @pl.when((index == 0) & (row < 2))
    def _():
        o_ref[...] = jnp.zeros_like(o_ref)

        @pl.when((row == 0) & (col == 0))
        def _():
            put(0, f_ref[3])

        @pl.when((row == 1) & (col == 0))
        def _():
            put(0, low10)

        @pl.when((row == 1) & (col == 1))
        def _():
            put(0, f_ref[4])


def factors(lead):
    edge = lead.shape[1]
    a00, a10, a11 = lead[0], lead[1], lead[2]
    identity = jnp.eye(edge, dtype=jnp.float32)

    def factor(block):
        low = jnp.linalg.cholesky(block)
        return low, jax.scipy.linalg.solve_triangular(low, identity, lower=True)

    low00, inv0 = factor(a00)
    low10 = mul_t(a10, inv0)
    low11, inv1 = factor(a11 - mul_t(low10, low10))
    return jnp.stack([inv0, low10, inv1, low00, low11])


def local(rows, cols, matrix):
    depth, _, edge, width, _, _ = matrix.shape
    parts = edge // LANES
    any_spec = pl.BlockSpec(memory_space=pl.ANY)
    vmem_spec = pl.BlockSpec(memory_space=pltpu.VMEM)
    dma = pltpu.SemaphoreType.DMA
    share = depth // 2
    f32 = jnp.float32
    panel, wide, lead = pl.pallas_call(
        functools.partial(exchange, rows, cols, depth),
        out_shape=(
            jax.ShapeDtypeStruct((2, depth, edge, parts, LANES), f32),
            jax.ShapeDtypeStruct((2, edge, width, parts, LANES), f32),
            jax.ShapeDtypeStruct((3, edge, parts, LANES), f32),
        ),
        in_specs=[any_spec],
        out_specs=(vmem_spec, vmem_spec, vmem_spec),
        scratch_shapes=[
            dma((4, share + 1)), dma((4, share + 1)), dma((3, rows - 1)), dma((3,)),
            dma((2, rows - 1)), dma((2,)), dma((7,)),
        ],
        compiler_params=pltpu.CompilerParams(collective_id=0, has_side_effects=True),
        name="exchange",
    )(matrix.reshape(depth, edge, width, parts, LANES))
    found = factors(lead.reshape(3, edge, edge))
    lines = edge * width * parts
    result = pl.pallas_call(
        functools.partial(update, width, edge),
        grid=(depth,),
        out_shape=jax.ShapeDtypeStruct((depth, lines, LANES), f32),
        in_specs=[
            pl.BlockSpec((2, 1, edge * parts, LANES), lambda i: (0, i, 0, 0)),
            vmem_spec,
            vmem_spec,
            pl.BlockSpec((1, lines, LANES), lambda i: (i, 0, 0)),
        ],
        out_specs=pl.BlockSpec((1, lines, LANES), lambda i: (i, 0, 0)),
        scratch_shapes=[pltpu.VMEM((2 * edge, width * edge), jnp.bfloat16)] * 2,
        compiler_params=pltpu.CompilerParams(vmem_limit_bytes=48 * 1024 * 1024),
        name="update",
    )(panel.reshape(2, depth, edge * parts, LANES), wide.reshape(2, lines, LANES), found,
      matrix.reshape(depth, lines, LANES))
    return result.reshape(matrix.shape)


def solution(mesh):
    spec = P(None, "row", None, None, "col", None)
    body = functools.partial(local, mesh.shape["row"], mesh.shape["col"])
    return jax.shard_map(body, mesh=mesh, in_specs=(spec,), out_specs=spec, check_vma=False)
```

```python
import functools

import jax
import jax.numpy as jnp
from jax import lax
from jax.experimental import pallas as pl
from jax.experimental.pallas import tpu as pltpu
from jax.sharding import PartitionSpec as P

LANES = 128
PIECES = 4
MESH_ID = pl.DeviceIdType.MESH
EXACT = lax.Precision.HIGHEST


def exchange(rows, cols, depth, p_ref, m_ref, r_ref, c_ref, l_ref, ring_send, ring_recv,
             lead_send, lead_recv, wide_send, wide_recv, own_sem):
    row = lax.axis_index("row")
    col = lax.axis_index("col")
    half = cols // 2
    odd = lax.rem(col, 2)
    place = jnp.where(odd == 0, col // 2, cols - 1 - col // 2)

    def at(place):
        place = lax.rem(place + cols, cols)
        return jnp.where(place < half, 2 * place, 2 * (cols - 1 - place) + 1)

    after, before = at(place + 1), at(place - 1)
    barrier = pltpu.get_barrier_semaphore()
    for step in range(1, rows):
        pl.semaphore_signal(barrier, inc=1, device_id=(lax.rem(row + step, rows), col),
                            device_id_type=MESH_ID)
    for peer in (after, before):
        pl.semaphore_signal(barrier, inc=1, device_id=(row, peer), device_id_type=MESH_ID)
    pl.semaphore_wait(barrier, rows + 1)

    leads = ((0, 0), (1, 0), (1, 1))

    def lead_copy(index, step):
        return pltpu.make_async_remote_copy(
            src_ref=p_ref.at[pl.ds(0, PIECES)], dst_ref=l_ref.at[index],
            send_sem=lead_send.at[index, step - 1], recv_sem=lead_recv.at[index],
            device_id=(lax.rem(row + step, rows), col), device_id_type=MESH_ID)

    def lead_own(index):
        return pltpu.make_async_copy(p_ref.at[pl.ds(0, PIECES)], l_ref.at[index], own_sem.at[index])

    for index, (lead_row, lead_col) in enumerate(leads):
        @pl.when((row == lead_row) & (col == lead_col))
        def _():
            for step in range(1, rows):
                lead_copy(index, step).start()
            lead_own(index).start()

    def wide_copy(which, step):
        return pltpu.make_async_remote_copy(
            src_ref=m_ref.at[0], dst_ref=c_ref.at[which],
            send_sem=wide_send.at[which, step - 1], recv_sem=wide_recv.at[which],
            device_id=(lax.rem(row + step, rows), col), device_id_type=MESH_ID)

    def wide_own(which):
        return pltpu.make_async_copy(m_ref.at[0], c_ref.at[which], own_sem.at[3 + which])

    def column_own(which):
        return pltpu.make_async_copy(p_ref, r_ref.at[which], own_sem.at[5 + which])

    for which in range(2):
        @pl.when(row == which)
        def _():
            for step in range(1, rows):
                wide_copy(which, step).start()
            wide_own(which).start()

        @pl.when(col == which)
        def _():
            column_own(which).start()

    for index, (lead_row, lead_col) in enumerate(leads):
        @pl.when((row != lead_row) & (col == lead_col))
        def _():
            lead_copy(index, 1).wait_recv()

        @pl.when((row == lead_row) & (col == lead_col))
        def _():
            lead_own(index).wait()

    streams = ((0, 1, 0), (0, -1, 1), (1, 1, 2), (1, -1, None))
    share = depth // 2 * PIECES
    total = share + PIECES

    def ring_copy(stream, piece, lead, first):
        source, way, block = streams[stream]
        if lead:
            src = dst = l_ref.at[block, piece]
        else:
            index = piece - PIECES + (share if way == -1 else 0)
            dst = r_ref.at[source, index]
            src = p_ref.at[index] if first else dst
        return pltpu.make_async_remote_copy(
            src_ref=src, dst_ref=dst, send_sem=ring_send.at[stream, piece],
            recv_sem=ring_recv.at[stream, piece],
            device_id=(row, after if way == 1 else before), device_id_type=MESH_ID)

    starts = (0, cols - 1)
    away = [lax.rem(way * (place - starts[source]) + cols, cols)
            for source, way, _ in streams]

    def serve(stream, piece, lead):
        @pl.when(away[stream] == 0)
        def _():
            ring_copy(stream, piece, lead, True).start()

        @pl.when(away[stream] > 0)
        def _():
            ring_copy(stream, piece, lead, False).wait_recv()

        @pl.when((away[stream] > 0) & (away[stream] < cols - 1))
        def _():
            ring_copy(stream, piece, lead, False).start()

    @pl.loop(0, total + cols - 1)
    def _(moment):
        for stream in range(len(streams)):
            piece = moment - away[stream]
            if streams[stream][2] is not None:
                @pl.when((piece >= 0) & (piece < PIECES))
                def _():
                    serve(stream, piece, True)

            @pl.when((piece >= PIECES) & (piece < total))
            def _():
                serve(stream, piece, False)

    for stream in range(len(streams)):
        @pl.when(away[stream] < cols - 1)
        def _():
            if streams[stream][2] is not None:
                @pl.loop(0, PIECES)
                def _(piece):
                    ring_copy(stream, piece, True, False).wait_send()

            @pl.loop(PIECES, total)
            def _(piece):
                ring_copy(stream, piece, False, False).wait_send()

    for index, (lead_row, lead_col) in enumerate(leads):
        @pl.when((row == lead_row) & (col == lead_col))
        def _():
            for step in range(1, rows):
                lead_copy(index, step).wait_send()

    for which in range(2):
        @pl.when(row == which)
        def _():
            for step in range(1, rows):
                wide_copy(which, step).wait_send()
            wide_own(which).wait()

        @pl.when(row != which)
        def _():
            wide_copy(which, 1).wait_recv()

        @pl.when(col == which)
        def _():
            column_own(which).wait()


def split(value):
    high = value.astype(jnp.bfloat16)
    return high, (value - high.astype(jnp.float32)).astype(jnp.bfloat16)


def mul(a, b):
    return jnp.dot(a, b, precision=EXACT, preferred_element_type=jnp.float32)


def mul_t(a, b):
    return lax.dot_general(a, b, (((1,), (1,)), ((), ())), precision=EXACT,
                           preferred_element_type=jnp.float32)


def update(width, edge, r_ref, c_ref, f_ref, m_ref, o_ref, stack_ref):
    index = pl.program_id(0)
    row = lax.axis_index("row")
    col = lax.axis_index("col")
    parts = edge // LANES
    stride = width * parts
    inv0, low10, inv1 = f_ref[0], f_ref[1], f_ref[2]

    def tile(ref, lead, j):
        return jnp.concatenate(
            [ref[lead + (pl.ds(j * parts + h, edge, stride=stride), slice(None))]
             for h in range(parts)], axis=1)

    def put(j, value):
        for h in range(parts):
            o_ref[0, pl.ds(j * parts + h, edge, stride=stride), :] = (
                value[:, h * LANES:(h + 1) * LANES])

    @pl.when(index == 0)
    def _():
        for j in range(width):
            first = mul(inv0, tile(c_ref, (0,), j))
            second = mul(inv1, tile(c_ref, (1,), j) - mul(low10, first))
            here = slice(j * edge, (j + 1) * edge)
            for k, value in enumerate((first, second)):
                high, low = split(value)
                for slot, half in enumerate((low, high, high)):
                    stack_ref[(2 * slot + k) * edge:(2 * slot + k + 1) * edge, here] = half

    first = mul_t(r_ref[0, 0], inv0)
    second = mul_t(r_ref[1, 0] - mul_t(first, low10), inv1)
    high, low = split(jnp.concatenate([first, second], axis=1))
    stack = jnp.concatenate([high, high, low], axis=1)
    for j in range(width):
        here = slice(j * edge, (j + 1) * edge)
        change = jnp.dot(stack, stack_ref[:, here], preferred_element_type=jnp.float32)
        put(j, tile(m_ref, (0,), j) - change)

    @pl.when(col == 0)
    def _():
        put(0, first)

    @pl.when(col == 1)
    def _():
        put(0, second)

    @pl.when((index == 0) & (row < 2))
    def _():
        o_ref[...] = jnp.zeros_like(o_ref)

        @pl.when((row == 0) & (col == 0))
        def _():
            put(0, f_ref[3])

        @pl.when((row == 1) & (col == 0))
        def _():
            put(0, low10)

        @pl.when((row == 1) & (col == 1))
        def _():
            put(0, f_ref[4])


def factor(block):
    half = block.shape[0] // 2
    identity = jnp.eye(half, dtype=jnp.float32)
    zero = jnp.zeros_like(identity)

    def one(part):
        low = jnp.linalg.cholesky(part)
        return low, jax.scipy.linalg.solve_triangular(low, identity, lower=True)

    top, inv_top = one(block[:half, :half])
    side = mul_t(block[half:, :half], inv_top)
    end, inv_end = one(block[half:, half:] - mul_t(side, side))
    corner = -mul(inv_end, mul(side, inv_top))
    return jnp.block([[top, zero], [side, end]]), jnp.block([[inv_top, zero], [corner, inv_end]])


def factors(lead):
    low00, inv0 = factor(lead[0])
    low10 = mul_t(lead[1], inv0)
    low11, inv1 = factor(lead[2] - mul_t(low10, low10))
    return jnp.stack([inv0, low10, inv1, low00, low11])


def local(rows, cols, matrix):
    depth, _, edge, width, _, _ = matrix.shape
    parts = edge // LANES
    any_spec = pl.BlockSpec(memory_space=pl.ANY)
    vmem_spec = pl.BlockSpec(memory_space=pltpu.VMEM)
    dma = pltpu.SemaphoreType.DMA
    total = (depth // 2 + 1) * PIECES
    lines = edge * width * parts
    f32 = jnp.float32
    panel, wide, lead = pl.pallas_call(
        functools.partial(exchange, rows, cols, depth),
        out_shape=(
            jax.ShapeDtypeStruct((2, depth * PIECES, edge // PIECES, edge), f32),
            jax.ShapeDtypeStruct((2, lines, LANES), f32),
            jax.ShapeDtypeStruct((3, PIECES, edge // PIECES, edge), f32),
        ),
        in_specs=[any_spec, any_spec],
        out_specs=(vmem_spec, vmem_spec, vmem_spec),
        scratch_shapes=[
            dma((4, total)), dma((4, total)), dma((3, rows - 1)), dma((3,)),
            dma((2, rows - 1)), dma((2,)), dma((7,)),
        ],
        compiler_params=pltpu.CompilerParams(collective_id=0, has_side_effects=True),
        name="exchange",
    )(matrix[:, 0, :, 0, 0, :].reshape(depth * PIECES, edge // PIECES, edge), matrix.reshape(depth, lines, LANES))
    found = factors(lead.reshape(3, edge, edge))
    result = pl.pallas_call(
        functools.partial(update, width, edge),
        grid=(depth,),
        out_shape=jax.ShapeDtypeStruct((depth, lines, LANES), f32),
        in_specs=[
            pl.BlockSpec((2, 1, edge, edge), lambda i: (0, i, 0, 0)),
            vmem_spec,
            vmem_spec,
            pl.BlockSpec((1, lines, LANES), lambda i: (i, 0, 0)),
        ],
        out_specs=pl.BlockSpec((1, lines, LANES), lambda i: (i, 0, 0)),
        scratch_shapes=[pltpu.VMEM((6 * edge, width * edge), jnp.bfloat16)],
        compiler_params=pltpu.CompilerParams(vmem_limit_bytes=48 * 1024 * 1024),
        name="update",
    )(panel.reshape(2, depth, edge, edge), wide, found,
      matrix.reshape(depth, lines, LANES))
    return result.reshape(matrix.shape)


def solution(mesh):
    spec = P(None, "row", None, None, "col", None)
    body = functools.partial(local, mesh.shape["row"], mesh.shape["col"])
    return jax.shard_map(body, mesh=mesh, in_specs=(spec,), out_specs=spec, check_vma=False)
```

```python
import functools

import jax
import jax.numpy as jnp
from jax import lax
from jax.experimental import pallas as pl
from jax.experimental.pallas import tpu as pltpu
from jax.sharding import PartitionSpec as P

LANES = 128
PIECES = 4
MESH_ID = pl.DeviceIdType.MESH
EXACT = lax.Precision.HIGHEST


def exchange(rows, cols, depth, p_ref, m_ref, r_ref, c_ref, l_ref, ring_send, ring_recv,
             lead_send, lead_recv, wide_send, wide_recv, own_sem):
    row = lax.axis_index("row")
    col = lax.axis_index("col")
    half = cols // 2
    odd = lax.rem(col, 2)
    place = jnp.where(odd == 0, col // 2, cols - 1 - col // 2)

    def at(place):
        place = lax.rem(place + cols, cols)
        return jnp.where(place < half, 2 * place, 2 * (cols - 1 - place) + 1)

    after, before = at(place + 1), at(place - 1)
    barrier = pltpu.get_barrier_semaphore()
    for step in range(1, rows):
        pl.semaphore_signal(barrier, inc=1, device_id=(lax.rem(row + step, rows), col),
                            device_id_type=MESH_ID)
    for peer in (after, before):
        pl.semaphore_signal(barrier, inc=1, device_id=(row, peer), device_id_type=MESH_ID)
    pl.semaphore_wait(barrier, rows + 1)

    leads = ((0, 0), (1, 0), (1, 1))

    def lead_copy(index, step):
        return pltpu.make_async_remote_copy(
            src_ref=p_ref.at[pl.ds(0, PIECES)], dst_ref=l_ref.at[index],
            send_sem=lead_send.at[index, step - 1], recv_sem=lead_recv.at[index],
            device_id=(lax.rem(row + step, rows), col), device_id_type=MESH_ID)

    def lead_own(index):
        return pltpu.make_async_copy(p_ref.at[pl.ds(0, PIECES)], l_ref.at[index], own_sem.at[index])

    for index, (lead_row, lead_col) in enumerate(leads):
        @pl.when((row == lead_row) & (col == lead_col))
        def _():
            for step in range(1, rows):
                lead_copy(index, step).start()
            lead_own(index).start()

    def wide_copy(which, step):
        return pltpu.make_async_remote_copy(
            src_ref=m_ref.at[0], dst_ref=c_ref.at[which],
            send_sem=wide_send.at[which, step - 1], recv_sem=wide_recv.at[which],
            device_id=(lax.rem(row + step, rows), col), device_id_type=MESH_ID)

    def wide_own(which):
        return pltpu.make_async_copy(m_ref.at[0], c_ref.at[which], own_sem.at[3 + which])

    def column_own():
        return pltpu.make_async_copy(p_ref, r_ref, own_sem.at[5])

    for which in range(2):
        @pl.when(row == which)
        def _():
            for step in range(1, rows):
                wide_copy(which, step).start()
            wide_own(which).start()

    @pl.when(col == 0)
    def _():
        column_own().start()

    for index, (lead_row, lead_col) in enumerate(leads):
        @pl.when((row != lead_row) & (col == lead_col))
        def _():
            lead_copy(index, 1).wait_recv()

        @pl.when((row == lead_row) & (col == lead_col))
        def _():
            lead_own(index).wait()

    streams = ((0, 1, 0), (0, -1, 1), (1, 1, 2))
    share = depth // 2 * PIECES
    total = share + PIECES

    def ring_copy(stream, piece, lead, first):
        source, way, block = streams[stream]
        if lead:
            src = dst = l_ref.at[block, piece]
        else:
            index = piece - PIECES + (share if way == -1 else 0)
            dst = r_ref.at[index]
            src = p_ref.at[index] if first else dst
        return pltpu.make_async_remote_copy(
            src_ref=src, dst_ref=dst, send_sem=ring_send.at[stream, piece],
            recv_sem=ring_recv.at[stream, piece],
            device_id=(row, after if way == 1 else before), device_id_type=MESH_ID)

    starts = (0, cols - 1)
    away = [lax.rem(way * (place - starts[source]) + cols, cols)
            for source, way, _ in streams]

    def serve(stream, piece, lead):
        @pl.when(away[stream] == 0)
        def _():
            ring_copy(stream, piece, lead, True).start()

        @pl.when(away[stream] > 0)
        def _():
            ring_copy(stream, piece, lead, False).wait_recv()

        @pl.when((away[stream] > 0) & (away[stream] < cols - 1))
        def _():
            ring_copy(stream, piece, lead, False).start()

    @pl.loop(0, total + cols - 1)
    def _(moment):
        for stream in range(len(streams)):
            piece = moment - away[stream]

            @pl.when((piece >= 0) & (piece < PIECES))
            def _():
                serve(stream, piece, True)

            if streams[stream][0] == 0:
                @pl.when((piece >= PIECES) & (piece < total))
                def _():
                    serve(stream, piece, False)

    for stream in range(len(streams)):
        @pl.when(away[stream] < cols - 1)
        def _():
            @pl.loop(0, PIECES)
            def _(piece):
                ring_copy(stream, piece, True, False).wait_send()

            if streams[stream][0] == 0:
                @pl.loop(PIECES, total)
                def _(piece):
                    ring_copy(stream, piece, False, False).wait_send()

    for index, (lead_row, lead_col) in enumerate(leads):
        @pl.when((row == lead_row) & (col == lead_col))
        def _():
            for step in range(1, rows):
                lead_copy(index, step).wait_send()

    for which in range(2):
        @pl.when(row == which)
        def _():
            for step in range(1, rows):
                wide_copy(which, step).wait_send()
            wide_own(which).wait()

        @pl.when(row != which)
        def _():
            wide_copy(which, 1).wait_recv()

    @pl.when(col == 0)
    def _():
        column_own().wait()


def split(value):
    high = value.astype(jnp.bfloat16)
    return high, (value - high.astype(jnp.float32)).astype(jnp.bfloat16)


def mul(a, b):
    return jnp.dot(a, b, precision=EXACT, preferred_element_type=jnp.float32)


def mul_t(a, b):
    return lax.dot_general(a, b, (((1,), (1,)), ((), ())), precision=EXACT,
                           preferred_element_type=jnp.float32)


def short(a, b, dim):
    (a_high, a_low), (b_high, b_low) = split(a), split(b)

    def dot(x, y):
        return lax.dot_general(x, y, (((1,), (dim,)), ((), ())),
                               preferred_element_type=jnp.float32)

    return dot(a_high, b_low) + dot(a_low, b_high) + dot(a_high, b_high)


def update(width, edge, r_ref, s_ref, c_ref, f_ref, m_ref, o_ref, stack_ref):
    index = pl.program_id(0)
    row = lax.axis_index("row")
    col = lax.axis_index("col")
    parts = edge // LANES
    stride = width * parts
    inv0, low10, inv1 = f_ref[0], f_ref[1], f_ref[2]

    def tile(ref, lead, j):
        return jnp.concatenate(
            [ref[lead + (pl.ds(j * parts + h, edge, stride=stride), slice(None))]
             for h in range(parts)], axis=1)

    def put(j, value):
        for h in range(parts):
            o_ref[0, pl.ds(j * parts + h, edge, stride=stride), :] = (
                value[:, h * LANES:(h + 1) * LANES])

    @pl.when(index == 0)
    def _():
        for j in range(width):
            first = short(inv0, tile(c_ref, (0,), j), 0)
            second = short(inv1, tile(c_ref, (1,), j) - short(low10, first, 0), 0)
            here = slice(j * edge, (j + 1) * edge)
            for k, value in enumerate((first, second)):
                high, low = split(value)
                for slot, half in enumerate((low, high, high)):
                    stack_ref[(2 * slot + k) * edge:(2 * slot + k + 1) * edge, here] = half

    first = short(r_ref[0], inv0, 1)
    second = short(s_ref[0] - short(first, low10, 1), inv1, 1)
    high, low = split(jnp.concatenate([first, second], axis=1))
    stack = jnp.concatenate([high, high, low], axis=1)
    for j in range(width):
        here = slice(j * edge, (j + 1) * edge)
        change = jnp.dot(stack, stack_ref[:, here], preferred_element_type=jnp.float32)
        put(j, tile(m_ref, (0,), j) - change)

    @pl.when(col == 0)
    def _():
        put(0, first)

    @pl.when(col == 1)
    def _():
        put(0, second)

    @pl.when((index == 0) & (row < 2))
    def _():
        o_ref[...] = jnp.zeros_like(o_ref)

        @pl.when((row == 0) & (col == 0))
        def _():
            put(0, f_ref[3])

        @pl.when((row == 1) & (col == 0))
        def _():
            put(0, low10)

        @pl.when((row == 1) & (col == 1))
        def _():
            put(0, f_ref[4])


def factor(block):
    half = block.shape[0] // 2
    identity = jnp.eye(half, dtype=jnp.float32)
    zero = jnp.zeros_like(identity)

    def one(part):
        low = jnp.linalg.cholesky(part)
        return low, jax.scipy.linalg.solve_triangular(low, identity, lower=True)

    top, inv_top = one(block[:half, :half])
    side = mul_t(block[half:, :half], inv_top)
    end, inv_end = one(block[half:, half:] - mul_t(side, side))
    corner = -mul(inv_end, mul(side, inv_top))
    return jnp.block([[top, zero], [side, end]]), jnp.block([[inv_top, zero], [corner, inv_end]])


def factors(lead):
    low00, inv0 = factor(lead[0])
    low10 = mul_t(lead[1], inv0)
    low11, inv1 = factor(lead[2] - mul_t(low10, low10))
    return jnp.stack([inv0, low10, inv1, low00, low11])


def local(rows, cols, matrix):
    depth, _, edge, width, _, _ = matrix.shape
    parts = edge // LANES
    any_spec = pl.BlockSpec(memory_space=pl.ANY)
    vmem_spec = pl.BlockSpec(memory_space=pltpu.VMEM)
    dma = pltpu.SemaphoreType.DMA
    total = (depth // 2 + 1) * PIECES
    lines = edge * width * parts
    f32 = jnp.float32
    column = matrix[:, 0, :, 0, 0, :]
    other = lax.psum(jnp.where(lax.axis_index("col") == 1, column, 0), "col")
    panel, wide, lead = pl.pallas_call(
        functools.partial(exchange, rows, cols, depth),
        out_shape=(
            jax.ShapeDtypeStruct((depth * PIECES, edge // PIECES, edge), f32),
            jax.ShapeDtypeStruct((2, lines, LANES), f32),
            jax.ShapeDtypeStruct((3, PIECES, edge // PIECES, edge), f32),
        ),
        in_specs=[any_spec, any_spec],
        out_specs=(vmem_spec, vmem_spec, vmem_spec),
        scratch_shapes=[
            dma((3, total)), dma((3, total)), dma((3, rows - 1)), dma((3,)),
            dma((2, rows - 1)), dma((2,)), dma((6,)),
        ],
        compiler_params=pltpu.CompilerParams(collective_id=0, has_side_effects=True),
        name="exchange",
    )(column.reshape(depth * PIECES, edge // PIECES, edge), matrix.reshape(depth, lines, LANES))
    found = factors(lead.reshape(3, edge, edge))
    result = pl.pallas_call(
        functools.partial(update, width, edge),
        grid=(depth,),
        out_shape=jax.ShapeDtypeStruct((depth, lines, LANES), f32),
        in_specs=[
            pl.BlockSpec((1, edge, edge), lambda i: (i, 0, 0)),
            pl.BlockSpec((1, edge, edge), lambda i: (i, 0, 0)),
            vmem_spec,
            vmem_spec,
            pl.BlockSpec((1, lines, LANES), lambda i: (i, 0, 0)),
        ],
        out_specs=pl.BlockSpec((1, lines, LANES), lambda i: (i, 0, 0)),
        scratch_shapes=[pltpu.VMEM((6 * edge, width * edge), jnp.bfloat16)],
        compiler_params=pltpu.CompilerParams(vmem_limit_bytes=48 * 1024 * 1024),
        name="update",
    )(panel.reshape(depth, edge, edge), other, wide, found,
      matrix.reshape(depth, lines, LANES))
    return result.reshape(matrix.shape)


def solution(mesh):
    spec = P(None, "row", None, None, "col", None)
    body = functools.partial(local, mesh.shape["row"], mesh.shape["col"])
    return jax.shard_map(body, mesh=mesh, in_specs=(spec,), out_specs=spec, check_vma=False)
```
